32 devices in a mesh: scene: 2 (over x), tile: 8 (over z, y), chan: 2 (over core).
Axes of the slice: x: 2, y: 2, z: 4, core: 2. Of those that a mesh axis runs over, the one named last changes fastest.
Arguments:
- raw_echoes: bfloat16 [256, 12, 2, 2048], P(('scene', 'tile'), 'chan'), parts along dimension 0, may hold values from -6 to 6
- range_taps: bfloat16 [12, 2, 512], replicated, may hold values from -0.1875 to 0.1875
- beam_weights: bfloat16 [12, 2, 2048], replicated, may hold values from -1.1953125 to 1.1953125
- channel_order: int32 [12], replicated, may hold values from 0 to 11, each once
- group_cells: int32 [8], replicated, may hold values from 128 to 384, as said below
- tap_counts: int32 [2048], replicated, may hold values from 384 to 640, as said below
- chirp_rates: float32 [2048], replicated, may hold values from 0.5 to 2
Outputs:
- focused_image: float32 [6144, 2, 128], P(('scene', 'tile', 'chan')), parts along dimension 0
The draws below stay inside these ranges and needn't reach their ends.
There are 2 independent parts, one for each index of `scene`. The reference program is written for one: setup_inputs(seed, part) draws one part's arguments, and reference() takes and returns one part's arrays. A program takes and returns all parts, laid end to end along the dimension named above; an argument that names none is the same for every part. Nothing has to cross between parts.
Inputs may be any that keep to these rules, and one draw needn't show every extreme that they name: `channel_order`: A permutation of the channels. `group_cells`: the counts sum to 2048; devices 2i and 2i + 1 of tile together own 2 * 256 cells; at least one device owns exactly 384. `tap_counts`: the first range cell has 384 taps and the last 640; counts rise with range up to a small jitter.
All inputs are finite; a program needn't handle non-finite values.
Results may differ from the reference program's by a relative error of at most 0.0053.
Values may be sent and summed in bfloat16 or wider, within the bound.
A program may use at most 320 MiB of HBM per device.

```python
import math
import jax
import jax.numpy as jnp
from jax import lax

R = 2048
C = 12
L = 512
KMAX = 640
KMIN = 384
PUL_DEV = 16
P_SIZE = 128
CH_DEV = 6
SHARE = 256
MAXG = 384
SLOTS = 3072
N_TILE = 8
N_CHAN = 2


def draw_group_cells(key, part):
    average = R // N_TILE
    couples = N_TILE // 2
    key_spread = jax.random.fold_in(key, 11)
    key_widest = jax.random.fold_in(key, 12)
    key_orient = jax.random.fold_in(key, 13)
    spread = jax.random.randint(key_spread, (couples,), 0, average // 2 + 1)
    widest = jax.random.randint(key_widest, (), 0, couples)
    spread = jnp.where(jnp.arange(couples) == widest, average // 2, spread)
    orient = jax.random.randint(key_orient, (couples,), 0, 2) * 2 - 1
    leading_cells = average + orient * spread
    trailing_cells = average - orient * spread
    return jnp.stack([leading_cells, trailing_cells], 1).reshape(N_TILE).astype(jnp.int32)


def draw_tap_counts(key, part):
    position = jnp.arange(R, dtype=jnp.int32)
    tap_span = KMAX - KMIN
    slope_base = KMIN + tap_span * position // max(R - 1, 1)
    jitter_reach = max(tap_span // 32, 1)
    jitter = jax.random.randint(jax.random.fold_in(key, 21), (R,), -jitter_reach, jitter_reach + 1)
    interior = (position > 0) & (position < R - 1)
    jitter = jnp.where(interior, jitter, 0)
    return jnp.clip(slope_base + jitter, KMIN, KMAX).astype(jnp.int32)


def levels(own_key, shape, split, low, largest):
    def one(dim, shards_of):
        draws = jax.random.uniform(jax.random.fold_in(jax.random.fold_in(own_key, 6), dim), (shards_of,), jnp.float32, low / len(split), largest / len(split))
        return jnp.repeat(jnp.exp(draws), shape[dim] // shards_of).reshape((-1,) + (1,) * (len(shape) - dim - 1))

    gain = one(*split[0])
    for cut in split[1:]:
        gain = gain * one(*cut)
    return gain


def noise(own_key, shape, width, most, split=(), kind=jnp.bfloat16):
    drawn = jax.random.normal(own_key, shape, jnp.float32) * width
    if len(split) > 0:
        drawn = levels(own_key, shape, split, -0.22, 0.18) * drawn
    return jnp.clip(drawn, min=-most, max=most).astype(kind)


def setup_inputs(seed: int = 0, part: int = 0) -> dict:
    keys = jax.random.split(jax.random.key(seed), 8)
    part_splits = jax.random.split(jax.random.fold_in(keys[7], part), 8)
    raw_echoes = noise(part_splits[0], (P_SIZE, C, 2, R), 1.0, 6.0, ((0, 8), (1, 2)))
    range_taps = noise(keys[1], (C, 2, L), (2 * L) ** -0.5, 0.1875)
    beam_weights = noise(keys[2], (C, 2, R), 0.2, 1.1953125)
    channel_order = jax.random.permutation(keys[3], C).astype(jnp.int32)
    group_cells = draw_group_cells(jax.random.fold_in(keys[7], 71), part)
    tap_counts = draw_tap_counts(jax.random.fold_in(keys[7], 71), part)
    chirp_rates = jnp.clip(jnp.exp(jax.random.uniform(keys[6], (R,), jnp.float32, math.log(0.5), math.log(2.0))), 0.5, 2.0)
    return {"raw_echoes": raw_echoes, "range_taps": range_taps, "beam_weights": beam_weights, "channel_order": channel_order, "group_cells": group_cells, "tap_counts": tap_counts, "chirp_rates": chirp_rates}


def toeplitz_rows(coeffs, block_len, span_len):
    leading = coeffs.shape[:-1]
    filler = jnp.zeros(leading + (span_len + 1 - coeffs.shape[-1],), coeffs.dtype)
    extended = jnp.concatenate([coeffs, filler], -1)
    repeated = jnp.tile(extended, (1,) * len(leading) + (block_len,))
    return repeated[..., :block_len * span_len].reshape(leading + (block_len, span_len))

def complex_matrix(toeplitz_pair):
    real_part = toeplitz_pair[..., 0, :, :]
    imag_part = toeplitz_pair[..., 1, :, :]
    from_real = jnp.stack([real_part, imag_part], -3)
    from_imag = jnp.stack([-imag_part, real_part], -3)
    return jnp.stack([from_real, from_imag], -4)

def block_windows(signal, block_len, lead_blocks, span_blocks, out_blocks):
    total_blocks = out_blocks + span_blocks - 1
    right_pad = total_blocks * block_len - lead_blocks * block_len - signal.shape[-1]
    padded = jnp.pad(signal, [(0, 0)] * (signal.ndim - 1) + [(lead_blocks * block_len, right_pad)])
    blocked = padded.reshape(signal.shape[:-1] + (total_blocks, block_len))
    return jnp.concatenate([blocked[..., offset_block:offset_block + out_blocks, :] for offset_block in range(span_blocks)], -1)

def chirp_taps(counts, sweep_rates, longest):
    position = jnp.arange(longest, dtype=jnp.int32)[None, :]
    lengths = counts[:, None]
    shifted = position - (longest // 2 - lengths // 2)
    inside = (shifted >= 0) & (shifted < lengths)
    extent = lengths.astype(jnp.float32)
    located = shifted.astype(jnp.float32)
    centred = (located - 0.5 * (extent - 1.0)) / extent
    angles = jnp.pi * sweep_rates[:, None] * extent * centred * centred
    envelope = (0.5 - 0.5 * jnp.cos(2.0 * jnp.pi * (located + 0.5) / extent)) * 1.6 / jnp.sqrt(extent)
    envelope = jnp.where(inside, envelope, jnp.zeros_like(envelope))
    return jnp.stack([envelope * jnp.cos(angles), envelope * jnp.sin(angles)], 1)

def azimuth_focus(columns, coeffs):
    block_len = coeffs.shape[-1] // 8
    pulses = columns.shape[-1]
    out_blocks = -(-pulses // block_len)
    windows = block_windows(columns, block_len, 4, 9, out_blocks)
    matrices = complex_matrix(toeplitz_rows(coeffs, block_len, 9 * block_len))
    product = jnp.einsum('sanw,saeiw->seni', windows, matrices)
    return product.reshape(columns.shape[:-1] + (out_blocks * block_len,))[..., :pulses]

def reference(raw_echoes, range_taps, beam_weights, channel_order, group_cells, tap_counts, chirp_rates):
    filters = jnp.take(range_taps, channel_order, axis=0).astype(jnp.float32)
    weights = jnp.take(beam_weights, channel_order, axis=0).astype(jnp.float32)
    block_len = L // 2
    matrices = complex_matrix(toeplitz_rows(filters, block_len, 3 * block_len))

    def pulse_block(echoes):
        windows = block_windows(echoes.astype(jnp.float32), block_len, 1, 3, R // block_len)
        spectra = jnp.einsum('pcanw,caeiw->pceni', windows, matrices).reshape(echoes.shape)
        real_term = spectra[:, :, 0] * weights[:, 0] - spectra[:, :, 1] * weights[:, 1]
        imag_term = spectra[:, :, 0] * weights[:, 1] + spectra[:, :, 1] * weights[:, 0]
        channel_terms = jnp.stack([real_term, imag_term], 2)
        grouped = lax.optimization_barrier(jnp.sum(channel_terms.reshape(channel_terms.shape[0], N_CHAN, CH_DEV, 2, R), 2))
        grouped = lax.optimization_barrier(grouped.astype(jnp.bfloat16)).astype(jnp.float32)
        return lax.optimization_barrier(jnp.sum(grouped, 1)).astype(jnp.bfloat16)
    beamed = lax.map(pulse_block, raw_echoes.reshape(N_TILE, PUL_DEV, C, 2, R)).reshape(P_SIZE, 2, R)
    columns = beamed.transpose(2, 1, 0)
    all_taps = chirp_taps(tap_counts, chirp_rates, KMAX).astype(jnp.bfloat16)

    def cell_block(cell_group):
        return azimuth_focus(cell_group[0].astype(jnp.float32), cell_group[1].astype(jnp.float32))
    focused = lax.map(cell_block, (columns.reshape(R // SHARE, SHARE, 2, P_SIZE), all_taps.reshape(R // SHARE, SHARE, 2, KMAX))).reshape(R, 2, P_SIZE)
    group_starts = (jnp.cumsum(group_cells) - group_cells).astype(jnp.int32)
    padded = jnp.pad(focused, ((0, MAXG), (0, 0), (0, 0)))

    def one_group(start_cell, size_cells):
        window_cut = lax.dynamic_slice_in_dim(padded, start_cell, MAXG, 0)
        inside = jnp.arange(MAXG, dtype=jnp.int32) < size_cells
        return jnp.where(inside[:, None, None], window_cut, jnp.zeros_like(window_cut))
    return jax.vmap(one_group)(group_starts, group_cells).reshape(SLOTS, 2, P_SIZE)
```

```python
import functools

import jax
import jax.numpy as jnp
import numpy as np
from jax import lax
from jax.experimental import pallas as pl
from jax.experimental.pallas import tpu as pltpu
from jax.sharding import PartitionSpec as P

KMAX = 640


def toeplitz_rows(coeffs, block_len, span_len):
    leading = coeffs.shape[:-1]
    filler = jnp.zeros(leading + (span_len + 1 - coeffs.shape[-1],), coeffs.dtype)
    extended = jnp.concatenate([coeffs, filler], -1)
    repeated = jnp.tile(extended, (1,) * len(leading) + (block_len,))
    return repeated[..., : block_len * span_len].reshape(leading + (block_len, span_len))


def complex_matrix(toeplitz_pair):
    real_part = toeplitz_pair[..., 0, :, :]
    imag_part = toeplitz_pair[..., 1, :, :]
    from_real = jnp.stack([real_part, imag_part], -3)
    from_imag = jnp.stack([-imag_part, real_part], -3)
    return jnp.stack([from_real, from_imag], -4)


def block_windows(signal, block_len, lead_blocks, span_blocks, out_blocks):
    total_blocks = out_blocks + span_blocks - 1
    right_pad = total_blocks * block_len - lead_blocks * block_len - signal.shape[-1]
    padded = jnp.pad(signal, [(0, 0)] * (signal.ndim - 1) + [(lead_blocks * block_len, right_pad)])
    blocked = padded.reshape(signal.shape[:-1] + (total_blocks, block_len))
    return jnp.concatenate(
        [
            blocked[..., offset_block : offset_block + out_blocks, :]
            for offset_block in range(span_blocks)
        ],
        -1,
    )


def chirp_taps(counts, sweep_rates, longest):
    position = jnp.arange(longest, dtype=jnp.int32)[None, :]
    lengths = counts[:, None]
    shifted = position - (longest // 2 - lengths // 2)
    inside = (shifted >= 0) & (shifted < lengths)
    extent = lengths.astype(jnp.float32)
    located = shifted.astype(jnp.float32)
    centred = (located - 0.5 * (extent - 1.0)) / extent
    angles = jnp.pi * sweep_rates[:, None] * extent * centred * centred
    envelope = (
        (0.5 - 0.5 * jnp.cos(2.0 * jnp.pi * (located + 0.5) / extent)) * 1.6 / jnp.sqrt(extent)
    )
    envelope = jnp.where(inside, envelope, jnp.zeros_like(envelope))
    return jnp.stack([envelope * jnp.cos(angles), envelope * jnp.sin(angles)], 1)


def range_compress(echoes, filters):
    block_len = filters.shape[-1] // 2
    windows = block_windows(echoes, block_len, 1, 3, echoes.shape[-1] // block_len)
    matrices = complex_matrix(toeplitz_rows(filters, block_len, 3 * block_len))
    product = jnp.einsum(
        "pcanw,caeiw->pceni", windows, matrices, preferred_element_type=jnp.float32
    )
    return product.reshape(echoes.shape)


def azimuth_focus(columns, coeffs):
    block_len = coeffs.shape[-1] // 8
    pulses = columns.shape[-1]
    out_blocks = -(-pulses // block_len)
    windows = block_windows(columns, block_len, 4, 9, out_blocks)
    matrices = complex_matrix(toeplitz_rows(coeffs, block_len, 9 * block_len))
    product = jnp.einsum("sanw,saeiw->seni", windows, matrices, preferred_element_type=jnp.float32)
    return product.reshape(columns.shape[:-1] + (out_blocks * block_len,))[..., :pulses]


def owner_slots(signal, group_starts, group_sizes, offset, slot_width, margin):
    padded = jnp.pad(signal, [(0, 0)] * (signal.ndim - 1) + [(0, margin)])

    def one_group(start_cell, size_cells):
        window_cut = lax.dynamic_slice_in_dim(
            padded, start_cell + offset, slot_width, signal.ndim - 1
        )
        inside = jnp.arange(slot_width, dtype=jnp.int32) + offset < size_cells
        return jnp.where(inside, window_cut, jnp.zeros_like(window_cut))

    return jax.vmap(one_group)(group_starts, group_sizes)


def generic_device(
    raw_echoes, range_taps, beam_weights, channel_order, group_cells, tap_counts, chirp_rates
):
    local_chans = raw_echoes.shape[1]
    all_chans = range_taps.shape[0]
    first_slot = lax.axis_index("chan") * local_chans
    own_channels = lax.dynamic_slice_in_dim(channel_order, first_slot, local_chans)
    selector = (own_channels[:, None] == jnp.arange(all_chans, dtype=jnp.int32)[None, :]).astype(
        jnp.bfloat16
    )
    filters = jnp.dot(
        selector, range_taps.reshape(all_chans, -1), preferred_element_type=jnp.float32
    )
    filters = filters.astype(jnp.bfloat16).reshape(local_chans, 2, -1)
    weights = jnp.dot(
        selector, beam_weights.reshape(all_chans, -1), preferred_element_type=jnp.float32
    )
    weights = weights.reshape(local_chans, 2, -1)
    spectra = range_compress(raw_echoes, filters)
    real_sum = jnp.sum(spectra[:, :, 0] * weights[:, 0] - spectra[:, :, 1] * weights[:, 1], 1)
    imag_sum = jnp.sum(spectra[:, :, 0] * weights[:, 1] + spectra[:, :, 1] * weights[:, 0], 1)
    partial_value = jnp.stack([real_sum, imag_sum], 1)
    tile_count = group_cells.shape[0]
    cell_count = raw_echoes.shape[-1]
    average = cell_count // tile_count
    capacity = average + average // 2
    chan_ways = lax.axis_size("chan")
    half_cap = capacity // chan_ways
    group_starts = jnp.cumsum(group_cells) - group_cells
    chan_offset = lax.axis_index("chan") * half_cap
    summed = lax.psum(partial_value.astype(jnp.bfloat16), "chan")
    outgoing = owner_slots(summed, group_starts, group_cells, chan_offset, half_cap, capacity)
    outgoing = outgoing.transpose(0, 3, 2, 1)
    incoming = lax.all_to_all(outgoing, "tile", split_axis=0, concat_axis=3, tiled=True)
    columns = incoming[0]
    tile_here = lax.axis_index("tile")
    begin_cell = lax.dynamic_index_in_dim(group_starts, tile_here, keepdims=False)
    owned_cells = lax.dynamic_index_in_dim(group_cells, tile_here, keepdims=False)
    local_slot = chan_offset + jnp.arange(half_cap, dtype=jnp.int32)
    inside = local_slot < owned_cells
    count_table = jnp.pad(tap_counts, (0, capacity), mode="edge")
    rate_table = jnp.pad(chirp_rates, (0, capacity), mode="edge")
    count_here = lax.dynamic_slice_in_dim(count_table, begin_cell + chan_offset, half_cap)
    rate_here = lax.dynamic_slice_in_dim(rate_table, begin_cell + chan_offset, half_cap)
    taps_here = chirp_taps(count_here, rate_here, KMAX)
    taps_here = jnp.where(inside[:, None, None], taps_here, jnp.zeros_like(taps_here)).astype(
        jnp.bfloat16
    )
    return azimuth_focus(columns, taps_here)


MESH = pl.DeviceIdType.MESH
BLOCK = 256
SPAN = 3 * BLOCK


def split_bf16(matrix):
    high = matrix.astype(jnp.bfloat16)
    low = (matrix - high.astype(np.float64)).astype(jnp.bfloat16)
    return np.stack([high, low])


def fourier_tables(tiles, pulses):
    points = 2 * pulses
    local = pulses // tiles
    freq = np.arange(points)[:, None]
    unit = 2.0 * np.pi / points

    def rotation(index, sign):
        angle = unit * ((freq * index[None, :]) % points)
        return np.cos(angle), sign * np.sin(angle)

    cos_x, sin_x = rotation(np.arange(pulses), -1.0)
    forward = np.block([[cos_x, -sin_x], [sin_x, cos_x]])
    order = np.arange(2 * pulses).reshape(2, tiles, local).transpose(1, 0, 2).reshape(-1)
    forward = forward[:, order]
    cos_h, sin_h = rotation(pulses - np.arange(points), -1.0)
    taps = np.block([[cos_h, -sin_h], [sin_h, cos_h]])
    cos_y, sin_y = rotation(np.arange(pulses), 1.0)
    inverse = np.block([[cos_y, sin_y], [-sin_y, cos_y]]) / points
    return split_bf16(forward), split_bf16(taps), split_bf16(inverse)


def range_kernel(
    half_cap,
    order_ref,
    cells_ref,
    raw_ref,
    filter_ref,
    weight_ref,
    count_ref,
    rate_ref,
    packed_ref,
    table_ref,
    blocks,
    partial,
):
    chan = pl.program_id(0)
    out_blocks = raw_ref.shape[3] // BLOCK
    pulses = raw_ref.shape[2]

    @pl.when(chan == 0)
    def _():
        edge = jnp.zeros((2, pulses, BLOCK), jnp.bfloat16)
        blocks[:, 0] = edge
        blocks[:, out_blocks + 1] = edge
        partial[...] = jnp.zeros_like(partial)

    for block in range(out_blocks):
        blocks[:, block + 1] = raw_ref[0, :, :, block * BLOCK : (block + 1) * BLOCK]

    def toeplitz(part):
        row = jnp.broadcast_to(filter_ref[0, part : part + 1, :], (128, SPAN))
        top = pltpu.roll(row, 0, 1, stride=1, stride_axis=0).astype(jnp.bfloat16)
        low = jnp.concatenate([top[:, SPAN - 128 :], top[:, : SPAN - 128]], 1)
        return jnp.concatenate([top, low], 0)

    real_rows = toeplitz(0)
    imag_rows = toeplitz(1)
    total = None
    for step in range(3):
        at = (SPAN - BLOCK * step) % SPAN
        matrix = jnp.concatenate(
            [real_rows[:, at : at + BLOCK], imag_rows[:, at : at + BLOCK]], 1
        )
        window = blocks[:, step : step + out_blocks].reshape(2 * out_blocks * pulses, BLOCK)
        term = jnp.dot(window, matrix, preferred_element_type=jnp.float32)
        total = term if total is None else total + term
    half = out_blocks * pulses
    comp_real = total[:half, :BLOCK] - total[half:, BLOCK:]
    comp_imag = total[half:, :BLOCK] + total[:half, BLOCK:]
    for block in range(out_blocks):
        cells = slice(block * BLOCK, (block + 1) * BLOCK)
        weight_real = weight_ref[0, 0:1, cells].astype(jnp.float32)
        weight_imag = weight_ref[0, 1:2, cells].astype(jnp.float32)
        value_real = comp_real[block * pulses : (block + 1) * pulses]
        value_imag = comp_imag[block * pulses : (block + 1) * pulses]
        partial[0, block] += weight_real * value_real - weight_imag * value_imag
        partial[1, block] += weight_imag * value_real + weight_real * value_imag

    @pl.when(chan == pl.num_programs(0) - 1)
    def _():
        width = 2 * BLOCK
        for pair in range(out_blocks // 2):
            first = cells_ref[2 * pair]
            for part in range(2):
                values = jnp.concatenate(
                    [partial[part, 2 * pair], partial[part, 2 * pair + 1]], 1
                )
                packed_ref[0, 2 * pair, part] = values[:, :BLOCK].astype(jnp.bfloat16)
                packed_ref[1, 2 * pair, part] = pltpu.roll(values, width - half_cap, 1)[
                    :, :BLOCK
                ].astype(jnp.bfloat16)
                moved = pltpu.roll(values, width - first, 1)
                packed_ref[0, 2 * pair + 1, part] = moved[:, :BLOCK].astype(jnp.bfloat16)
                packed_ref[1, 2 * pair + 1, part] = pltpu.roll(moved, width - half_cap, 1)[
                    :, :BLOCK
                ].astype(jnp.bfloat16)
        tile_here = lax.axis_index("tile")
        offset = lax.axis_index("chan") * half_cap
        begin = offset
        for tile in range(cells_ref.shape[0]):
            begin += jnp.where(tile < tile_here, cells_ref[tile], 0)
        cell_count = count_ref.shape[1]
        shift = lax.rem(2 * cell_count - begin, cell_count)

        def own(table):
            spread = jnp.broadcast_to(table.astype(jnp.float32), (8, cell_count))
            return pltpu.roll(spread, shift, 1)[:, :BLOCK]

        extent = own(count_ref[...])
        slot = lax.broadcasted_iota(jnp.int32, (8, BLOCK), 1)
        live = (slot < half_cap) & (slot + offset < cells_ref[tile_here])
        scale = jnp.where(live, 1.6 / jnp.sqrt(extent), 0.0)
        table_ref[0] = extent
        table_ref[1] = own(rate_ref[...])
        table_ref[2] = scale


def range_call(raw_echoes, range_taps, beam_weights, order, cells, counts, rates, half_cap):
    local_chans = raw_echoes.shape[1]
    pulses = raw_echoes.shape[0]
    cell_count = raw_echoes.shape[3]
    tiles = cells.shape[0]
    out_blocks = cell_count // BLOCK
    taps = range_taps.shape[-1]
    echoes = raw_echoes.transpose(1, 2, 0, 3)
    reversed_taps = jnp.concatenate(
        [
            range_taps[..., :1],
            jnp.zeros(range_taps.shape[:2] + (SPAN - taps,), range_taps.dtype),
            jnp.flip(range_taps[..., 1:], -1),
        ],
        -1,
    ).astype(jnp.float32)

    def physical(chan, order_ref, cells_ref):
        return (order_ref[lax.axis_index("chan") * local_chans + chan], 0, 0)

    return pl.pallas_call(
        functools.partial(range_kernel, half_cap),
        grid_spec=pltpu.PrefetchScalarGridSpec(
            num_scalar_prefetch=2,
            grid=(local_chans,),
            in_specs=[
                pl.BlockSpec((1, 2, pulses, cell_count), lambda c, o, g: (c, 0, 0, 0)),
                pl.BlockSpec((1, 2, SPAN), physical),
                pl.BlockSpec((1, 2, cell_count), physical),
                pl.BlockSpec((1, cell_count), lambda c, o, g: (0, 0)),
                pl.BlockSpec((1, cell_count), lambda c, o, g: (0, 0)),
            ],
            out_specs=[
                pl.BlockSpec((2, tiles, 2, pulses, BLOCK), lambda c, o, g: (0, 0, 0, 0, 0)),
                pl.BlockSpec((3, 8, BLOCK), lambda c, o, g: (0, 0, 0)),
            ],
            scratch_shapes=[
                pltpu.VMEM((2, out_blocks + 2, pulses, BLOCK), jnp.bfloat16),
                pltpu.VMEM((2, out_blocks, pulses, BLOCK), jnp.float32),
            ],
        ),
        out_shape=[
            jax.ShapeDtypeStruct((2, tiles, 2, pulses, BLOCK), jnp.bfloat16),
            jax.ShapeDtypeStruct((3, 8, BLOCK), jnp.float32),
        ],
        compiler_params=pltpu.CompilerParams(vmem_limit_bytes=32 << 20),
    )(order, cells, echoes, reversed_taps, beam_weights, counts[None], rates[None])


def even_series(square, terms):
    value = jnp.full_like(square, terms[-1])
    for term in reversed(terms[:-1]):
        value = value * square + term
    return value


COS_TERMS = [(-1.0) ** n * (2 * np.pi) ** (2 * n) / float(np.prod(np.arange(1, 2 * n + 1, dtype=np.float64))) for n in range(9)]
SIN_TERMS = [(-1.0) ** n * (2 * np.pi) ** (2 * n + 1) / float(np.prod(np.arange(1, 2 * n + 2, dtype=np.float64))) for n in range(9)]


def write_taps(table_ref, tap_ref, first_tap):
    rows = tap_ref.shape[0] // 2
    extent = table_ref[0, 0:1]
    rate = table_ref[1, 0:1]
    scale = table_ref[2, 0:1]
    length = extent.astype(jnp.int32)
    start = KMAX // 2 - length // 2
    inverse = 1.0 / extent
    turn = 0.5 * rate * extent
    for at in range(0, rows, 32):
        tap = lax.broadcasted_iota(jnp.int32, (32, BLOCK), 0) + (first_tap + at)
        shifted = tap - start
        inside = (shifted >= 0) & (shifted < length)
        centred = (shifted.astype(jnp.float32) - 0.5 * (extent - 1.0)) * inverse
        square = centred * centred
        envelope = jnp.where(inside, scale * (0.5 + 0.5 * even_series(square, COS_TERMS)), 0.0)
        turns = turn * square
        turns = turns - jnp.floor(turns + 0.5)
        turn_square = turns * turns
        real = envelope * even_series(turn_square, COS_TERMS)
        imag = envelope * (turns * even_series(turn_square, SIN_TERMS))
        tap_ref[at : at + 32] = real.astype(jnp.bfloat16)
        tap_ref[rows + at : rows + at + 32] = imag.astype(jnp.bfloat16)


def azimuth_kernel(
    packed_ref,
    table_ref,
    forward_ref,
    spectrum_ref,
    inverse_ref,
    out_ref,
    other,
    beam,
    columns,
    tap_ref,
    pair_sems,
    send_sems,
    recv_sems,
):
    tiles = beam.shape[0]
    tile_here = lax.axis_index("tile")
    chan_here = lax.axis_index("chan")
    barrier = pltpu.get_barrier_semaphore()
    pl.semaphore_signal(barrier, inc=1, device_id={"chan": 1 - chan_here}, device_id_type=MESH)
    for hop in range(1, tiles):
        target = lax.rem(tile_here + hop, tiles)
        pl.semaphore_signal(barrier, inc=1, device_id={"tile": target}, device_id_type=MESH)
    pl.semaphore_wait(barrier, tiles)
    swap = pltpu.make_async_remote_copy(
        src_ref=packed_ref.at[1 - chan_here],
        dst_ref=other,
        send_sem=pair_sems.at[0],
        recv_sem=pair_sems.at[1],
        device_id={"chan": 1 - chan_here},
        device_id_type=MESH,
    )
    swap.start()
    pulses = out_ref.shape[1] // 2
    write_taps(table_ref, tap_ref, KMAX // 2 - pulses)
    swap.wait()
    beam[...] = (
        packed_ref[chan_here].astype(jnp.float32) + other[...].astype(jnp.float32)
    ).astype(jnp.bfloat16)
    copies = []
    for hop in range(1, tiles):
        target = lax.rem(tile_here + hop, tiles)
        copy = pltpu.make_async_remote_copy(
            src_ref=beam.at[target],
            dst_ref=columns.at[tile_here],
            send_sem=send_sems.at[hop],
            recv_sem=recv_sems.at[hop],
            device_id={"tile": target},
            device_id_type=MESH,
        )
        copy.start()
        copies.append(copy)
    columns[tile_here] = beam[tile_here]
    taps = tap_ref[...]
    response = jnp.dot(spectrum_ref[0], taps, preferred_element_type=jnp.float32) + jnp.dot(
        spectrum_ref[1], taps, preferred_element_type=jnp.float32
    )
    for copy in copies:
        copy.wait()
    signal = columns[...].reshape(2 * pulses, BLOCK)
    spectrum = jnp.dot(forward_ref[0], signal, preferred_element_type=jnp.float32) + jnp.dot(
        forward_ref[1], signal, preferred_element_type=jnp.float32
    )
    points = 2 * pulses
    real, imag = spectrum[:points], spectrum[points:]
    tap_real, tap_imag = response[:points], response[points:]
    product = jnp.concatenate(
        [real * tap_real - imag * tap_imag, real * tap_imag + imag * tap_real], 0
    )
    high = product.astype(jnp.bfloat16)
    low = (product - high.astype(jnp.float32)).astype(jnp.bfloat16)
    over = (((0,), (0,)), ((), ()))
    result = lax.dot_general(high, inverse_ref[0], over, preferred_element_type=jnp.float32)
    result += lax.dot_general(low, inverse_ref[0], over, preferred_element_type=jnp.float32)
    result += lax.dot_general(high, inverse_ref[1], over, preferred_element_type=jnp.float32)
    out_ref[...] = result[: out_ref.shape[0]]


def azimuth_call(packed, table, half_cap):
    _, tiles, _, local, _ = packed.shape
    pulses = tiles * local
    forward, spectrum, inverse = fourier_tables(tiles, pulses)
    vmem = pl.BlockSpec(memory_space=pltpu.VMEM)
    return pl.pallas_call(
        azimuth_kernel,
        out_shape=jax.ShapeDtypeStruct((half_cap, 2 * pulses), jnp.float32),
        in_specs=[vmem] * 5,
        out_specs=vmem,
        scratch_shapes=[
            pltpu.VMEM((tiles, 2, local, BLOCK), jnp.bfloat16),
            pltpu.VMEM((tiles, 2, local, BLOCK), jnp.bfloat16),
            pltpu.VMEM((tiles, 2, local, BLOCK), jnp.bfloat16),
            pltpu.VMEM((4 * pulses, BLOCK), jnp.bfloat16),
            pltpu.SemaphoreType.DMA((2,)),
            pltpu.SemaphoreType.DMA((tiles,)),
            pltpu.SemaphoreType.DMA((tiles,)),
        ],
        compiler_params=pltpu.CompilerParams(
            collective_id=0, has_side_effects=True, vmem_limit_bytes=32 << 20
        ),
    )(packed, table, jnp.asarray(forward), jnp.asarray(spectrum), jnp.asarray(inverse))


def on_device(
    raw_echoes, range_taps, beam_weights, channel_order, group_cells, tap_counts, chirp_rates
):
    tiles = group_cells.shape[0]
    local, _, _, cell_count = raw_echoes.shape
    average = cell_count // tiles
    half_cap = (average + average // 2) // lax.axis_size("chan")
    fits = average == BLOCK and lax.axis_size("chan") == 2 and 2 * tiles * local == BLOCK
    if not fits or range_taps.shape[-1] != 2 * BLOCK:
        return generic_device(
            raw_echoes,
            range_taps,
            beam_weights,
            channel_order,
            group_cells,
            tap_counts,
            chirp_rates,
        )
    packed, table = range_call(
        raw_echoes,
        range_taps,
        beam_weights,
        channel_order,
        group_cells,
        tap_counts,
        chirp_rates,
        half_cap,
    )
    image = azimuth_call(packed, table, half_cap)
    return image.reshape(half_cap, 2, tiles * local)


def solution(mesh):
    return jax.shard_map(
        on_device,
        mesh=mesh,
        in_specs=(P(("scene", "tile"), "chan", None, None), P(), P(), P(), P(), P(), P()),
        out_specs=P(("scene", "tile", "chan"), None, None),
        check_vma=False,
    )
```

```python
import functools

import jax
import jax.numpy as jnp
import numpy as np
from jax import lax
from jax.experimental import pallas as pl
from jax.experimental.pallas import tpu as pltpu
from jax.sharding import PartitionSpec as P

KMAX = 640


def toeplitz_rows(coeffs, block_len, span_len):
    leading = coeffs.shape[:-1]
    filler = jnp.zeros(leading + (span_len + 1 - coeffs.shape[-1],), coeffs.dtype)
    extended = jnp.concatenate([coeffs, filler], -1)
    repeated = jnp.tile(extended, (1,) * len(leading) + (block_len,))
    return repeated[..., : block_len * span_len].reshape(leading + (block_len, span_len))


def complex_matrix(toeplitz_pair):
    real_part = toeplitz_pair[..., 0, :, :]
    imag_part = toeplitz_pair[..., 1, :, :]
    from_real = jnp.stack([real_part, imag_part], -3)
    from_imag = jnp.stack([-imag_part, real_part], -3)
    return jnp.stack([from_real, from_imag], -4)


def block_windows(signal, block_len, lead_blocks, span_blocks, out_blocks):
    total_blocks = out_blocks + span_blocks - 1
    right_pad = total_blocks * block_len - lead_blocks * block_len - signal.shape[-1]
    padded = jnp.pad(signal, [(0, 0)] * (signal.ndim - 1) + [(lead_blocks * block_len, right_pad)])
    blocked = padded.reshape(signal.shape[:-1] + (total_blocks, block_len))
    return jnp.concatenate(
        [
            blocked[..., offset_block : offset_block + out_blocks, :]
            for offset_block in range(span_blocks)
        ],
        -1,
    )


def chirp_taps(counts, sweep_rates, longest):
    position = jnp.arange(longest, dtype=jnp.int32)[None, :]
    lengths = counts[:, None]
    shifted = position - (longest // 2 - lengths // 2)
    inside = (shifted >= 0) & (shifted < lengths)
    extent = lengths.astype(jnp.float32)
    located = shifted.astype(jnp.float32)
    centred = (located - 0.5 * (extent - 1.0)) / extent
    angles = jnp.pi * sweep_rates[:, None] * extent * centred * centred
    envelope = (
        (0.5 - 0.5 * jnp.cos(2.0 * jnp.pi * (located + 0.5) / extent)) * 1.6 / jnp.sqrt(extent)
    )
    envelope = jnp.where(inside, envelope, jnp.zeros_like(envelope))
    return jnp.stack([envelope * jnp.cos(angles), envelope * jnp.sin(angles)], 1)


def range_compress(echoes, filters):
    block_len = filters.shape[-1] // 2
    windows = block_windows(echoes, block_len, 1, 3, echoes.shape[-1] // block_len)
    matrices = complex_matrix(toeplitz_rows(filters, block_len, 3 * block_len))
    product = jnp.einsum(
        "pcanw,caeiw->pceni", windows, matrices, preferred_element_type=jnp.float32
    )
    return product.reshape(echoes.shape)


def azimuth_focus(columns, coeffs):
    block_len = coeffs.shape[-1] // 8
    pulses = columns.shape[-1]
    out_blocks = -(-pulses // block_len)
    windows = block_windows(columns, block_len, 4, 9, out_blocks)
    matrices = complex_matrix(toeplitz_rows(coeffs, block_len, 9 * block_len))
    product = jnp.einsum("sanw,saeiw->seni", windows, matrices, preferred_element_type=jnp.float32)
    return product.reshape(columns.shape[:-1] + (out_blocks * block_len,))[..., :pulses]


def owner_slots(signal, group_starts, group_sizes, offset, slot_width, margin):
    padded = jnp.pad(signal, [(0, 0)] * (signal.ndim - 1) + [(0, margin)])

    def one_group(start_cell, size_cells):
        window_cut = lax.dynamic_slice_in_dim(
            padded, start_cell + offset, slot_width, signal.ndim - 1
        )
        inside = jnp.arange(slot_width, dtype=jnp.int32) + offset < size_cells
        return jnp.where(inside, window_cut, jnp.zeros_like(window_cut))

    return jax.vmap(one_group)(group_starts, group_sizes)


def generic_device(
    raw_echoes, range_taps, beam_weights, channel_order, group_cells, tap_counts, chirp_rates
):
    local_chans = raw_echoes.shape[1]
    all_chans = range_taps.shape[0]
    first_slot = lax.axis_index("chan") * local_chans
    own_channels = lax.dynamic_slice_in_dim(channel_order, first_slot, local_chans)
    selector = (own_channels[:, None] == jnp.arange(all_chans, dtype=jnp.int32)[None, :]).astype(
        jnp.bfloat16
    )
    filters = jnp.dot(
        selector, range_taps.reshape(all_chans, -1), preferred_element_type=jnp.float32
    )
    filters = filters.astype(jnp.bfloat16).reshape(local_chans, 2, -1)
    weights = jnp.dot(
        selector, beam_weights.reshape(all_chans, -1), preferred_element_type=jnp.float32
    )
    weights = weights.reshape(local_chans, 2, -1)
    spectra = range_compress(raw_echoes, filters)
    real_sum = jnp.sum(spectra[:, :, 0] * weights[:, 0] - spectra[:, :, 1] * weights[:, 1], 1)
    imag_sum = jnp.sum(spectra[:, :, 0] * weights[:, 1] + spectra[:, :, 1] * weights[:, 0], 1)
    partial_value = jnp.stack([real_sum, imag_sum], 1)
    tile_count = group_cells.shape[0]
    cell_count = raw_echoes.shape[-1]
    average = cell_count // tile_count
    capacity = average + average // 2
    chan_ways = lax.axis_size("chan")
    half_cap = capacity // chan_ways
    group_starts = jnp.cumsum(group_cells) - group_cells
    chan_offset = lax.axis_index("chan") * half_cap
    summed = lax.psum(partial_value.astype(jnp.bfloat16), "chan")
    outgoing = owner_slots(summed, group_starts, group_cells, chan_offset, half_cap, capacity)
    outgoing = outgoing.transpose(0, 3, 2, 1)
    incoming = lax.all_to_all(outgoing, "tile", split_axis=0, concat_axis=3, tiled=True)
    columns = incoming[0]
    tile_here = lax.axis_index("tile")
    begin_cell = lax.dynamic_index_in_dim(group_starts, tile_here, keepdims=False)
    owned_cells = lax.dynamic_index_in_dim(group_cells, tile_here, keepdims=False)
    local_slot = chan_offset + jnp.arange(half_cap, dtype=jnp.int32)
    inside = local_slot < owned_cells
    count_table = jnp.pad(tap_counts, (0, capacity), mode="edge")
    rate_table = jnp.pad(chirp_rates, (0, capacity), mode="edge")
    count_here = lax.dynamic_slice_in_dim(count_table, begin_cell + chan_offset, half_cap)
    rate_here = lax.dynamic_slice_in_dim(rate_table, begin_cell + chan_offset, half_cap)
    taps_here = chirp_taps(count_here, rate_here, KMAX)
    taps_here = jnp.where(inside[:, None, None], taps_here, jnp.zeros_like(taps_here)).astype(
        jnp.bfloat16
    )
    return azimuth_focus(columns, taps_here)


MESH = pl.DeviceIdType.MESH
BLOCK = 256
SPAN = 3 * BLOCK


def split_bf16(matrix):
    high = matrix.astype(jnp.bfloat16)
    low = (matrix - high.astype(np.float64)).astype(jnp.bfloat16)
    return np.stack([high, low])


def fourier_tables(pulses):
    points = 2 * pulses
    freq = np.arange(points)[:, None]
    unit = 2.0 * np.pi / points

    def rotation(index, sign):
        angle = unit * ((freq * index[None, :]) % points)
        return np.cos(angle), sign * np.sin(angle)

    cos_x, sin_x = rotation(np.arange(pulses), -1.0)
    forward = np.block([[cos_x, -sin_x], [sin_x, cos_x]])
    order = np.arange(2 * pulses).reshape(2, pulses).T.reshape(-1)
    forward = forward[:, order]
    cos_h, sin_h = rotation(pulses - np.arange(points), -1.0)
    taps = np.block([[cos_h, -sin_h], [sin_h, cos_h]])
    cos_y, sin_y = rotation(np.arange(pulses), 1.0)
    inverse = np.block([[cos_y, sin_y], [-sin_y, cos_y]]) / points
    return split_bf16(forward), split_bf16(taps), split_bf16(inverse)


def even_series(square, terms):
    value = jnp.full_like(square, terms[-1])
    for term in reversed(terms[:-1]):
        value = value * square + term
    return value


COS_TERMS = [(-1.0) ** n * (2 * np.pi) ** (2 * n) / float(np.prod(np.arange(1, 2 * n + 1, dtype=np.float64))) for n in range(9)]
SIN_TERMS = [(-1.0) ** n * (2 * np.pi) ** (2 * n + 1) / float(np.prod(np.arange(1, 2 * n + 2, dtype=np.float64))) for n in range(9)]


def write_taps(extent, rate, scale, tap_ref, first_tap):
    rows = tap_ref.shape[0] // 2
    length = extent.astype(jnp.int32)
    start = KMAX // 2 - length // 2
    inverse = 1.0 / extent
    turn = 0.5 * rate * extent
    for at in range(0, rows, 32):
        tap = lax.broadcasted_iota(jnp.int32, (32, BLOCK), 0) + (first_tap + at)
        shifted = tap - start
        inside = (shifted >= 0) & (shifted < length)
        centred = (shifted.astype(jnp.float32) - 0.5 * (extent - 1.0)) * inverse
        square = centred * centred
        envelope = jnp.where(inside, scale * (0.5 + 0.5 * even_series(square, COS_TERMS)), 0.0)
        turns = turn * square
        turns = turns - jnp.floor(turns + 0.5)
        turn_square = turns * turns
        real = envelope * even_series(turn_square, COS_TERMS)
        imag = envelope * (turns * even_series(turn_square, SIN_TERMS))
        tap_ref[at : at + 32] = real.astype(jnp.bfloat16)
        tap_ref[rows + at : rows + at + 32] = imag.astype(jnp.bfloat16)


def focus_kernel(
    half_cap,
    order_ref,
    cells_ref,
    raw_ref,
    filter_ref,
    weight_ref,
    count_ref,
    rate_ref,
    forward_ref,
    spectrum_ref,
    inverse_ref,
    out_ref,
    raw,
    filters,
    weights,
    counts,
    rates,
    forward,
    spectrum,
    inverse,
    blocks,
    mirror,
    straight,
    crossed,
    packed,
    other,
    beam,
    columns,
    tap_ref,
    load_sems,
    raw_sems,
    pair_sems,
    send_sems,
    recv_sems,
):
    tiles = beam.shape[0]
    tile_here = lax.axis_index("tile")
    chan_here = lax.axis_index("chan")
    local_chans = raw.shape[0]
    out_blocks = blocks.shape[0] - 2
    rows = blocks.shape[1]
    slots, _, pulses = out_ref.shape
    points = 2 * pulses
    barrier = pltpu.get_barrier_semaphore()
    pl.semaphore_signal(barrier, inc=1, device_id={"chan": 1 - chan_here}, device_id_type=MESH)
    for hop in range(1, tiles):
        target = lax.rem(tile_here + hop, tiles)
        pl.semaphore_signal(barrier, inc=1, device_id={"tile": target}, device_id_type=MESH)

    def fetch(source, target, at):
        return pltpu.make_async_copy(source, target, load_sems.at[at])

    def fetch_raw(chan):
        return pltpu.make_async_copy(raw_ref.at[:, chan], raw.at[chan], raw_sems.at[chan])

    get_filters = fetch(filter_ref, filters, 0)
    get_weights = fetch(weight_ref, weights, 1)
    late = [
        fetch(count_ref, counts, 2),
        fetch(rate_ref, rates, 3),
        fetch(spectrum_ref, spectrum, 4),
        fetch(forward_ref, forward, 5),
        fetch(inverse_ref, inverse, 6),
    ]
    get_filters.start()
    get_weights.start()
    for chan in range(local_chans):
        fetch_raw(chan).start()
    for copy in late:
        copy.start()

    edge = jnp.zeros((rows, BLOCK), jnp.bfloat16)
    blocks[0] = edge
    blocks[out_blocks + 1] = edge
    straight[...] = jnp.zeros_like(straight)
    crossed[...] = jnp.zeros_like(crossed)
    row = lax.broadcasted_iota(jnp.int32, (BLOCK, BLOCK), 0)
    lane = lax.broadcasted_iota(jnp.int32, (BLOCK, BLOCK), 1)
    mirror[...] = jnp.where(row + lane == BLOCK - 1, 1.0, 0.0).astype(jnp.bfloat16)
    get_filters.wait()
    get_weights.wait()

    def one_channel(chan, carry):
        physical = order_ref[chan_here * local_chans + chan]
        own_filter = filters[physical]
        own_weight = weights[physical].astype(jnp.float32)
        fetch_raw(chan).wait()
        for block in range(out_blocks):
            cells = slice(block * BLOCK, (block + 1) * BLOCK)
            blocks[block + 1] = raw[chan, :, :, cells].reshape(rows, BLOCK)

        first_half = jnp.dot(
            own_filter[:, :BLOCK], mirror[...], preferred_element_type=jnp.float32
        )
        second_half = jnp.dot(
            own_filter[:, BLOCK:], mirror[...], preferred_element_type=jnp.float32
        )
        backward = jnp.concatenate([jnp.zeros_like(first_half), second_half, first_half], 1)

        def toeplitz(part):
            row = jnp.broadcast_to(backward[part : part + 1], (128, SPAN))
            top = pltpu.roll(row, 1, 1, stride=1, stride_axis=0).astype(jnp.bfloat16)
            low = jnp.concatenate([top[:, SPAN - 128 :], top[:, : SPAN - 128]], 1)
            return jnp.concatenate([top, low], 0)

        real_rows = toeplitz(0)
        imag_rows = toeplitz(1)
        total = None
        for step in range(3):
            at = (SPAN - BLOCK * step) % SPAN
            matrix = jnp.concatenate(
                [real_rows[:, at : at + BLOCK], imag_rows[:, at : at + BLOCK]], 1
            )
            window = blocks[step : step + out_blocks].reshape(out_blocks * rows, BLOCK)
            term = jnp.dot(window, matrix, preferred_element_type=jnp.float32)
            total = term if total is None else total + term
        for block in range(out_blocks):
            cells = slice(block * BLOCK, (block + 1) * BLOCK)
            weight_real = own_weight[0:1, cells]
            weight_imag = own_weight[1:2, cells]
            by_real = total[block * rows : (block + 1) * rows, :BLOCK]
            by_imag = total[block * rows : (block + 1) * rows, BLOCK:]
            straight[block] += weight_real * by_real - weight_imag * by_imag
            crossed[block] += weight_imag * by_real + weight_real * by_imag
        return carry

    lax.fori_loop(0, local_chans, one_channel, 0)

    width = 2 * BLOCK
    is_real = lax.broadcasted_iota(jnp.int32, (rows, BLOCK), 0) % 2 == 0

    def summed(block):
        turned = crossed[block]
        return straight[block] + jnp.where(
            is_real, -pltpu.roll(turned, rows - 1, 0), pltpu.roll(turned, 1, 0)
        )

    for pair in range(out_blocks // 2):
        first = cells_ref[2 * pair]
        values = jnp.concatenate([summed(2 * pair), summed(2 * pair + 1)], 1)
        moved = pltpu.roll(values, width - first, 1)
        packed[0, 2 * pair] = values[:, :BLOCK].astype(jnp.bfloat16)
        packed[0, 2 * pair + 1] = moved[:, :BLOCK].astype(jnp.bfloat16)
        values = pltpu.roll(values, width - half_cap, 1)
        moved = pltpu.roll(moved, width - half_cap, 1)
        packed[1, 2 * pair] = values[:, :BLOCK].astype(jnp.bfloat16)
        packed[1, 2 * pair + 1] = moved[:, :BLOCK].astype(jnp.bfloat16)

    pl.semaphore_wait(barrier, tiles)
    swap = pltpu.make_async_remote_copy(
        src_ref=packed.at[1 - chan_here],
        dst_ref=other,
        send_sem=pair_sems.at[0],
        recv_sem=pair_sems.at[1],
        device_id={"chan": 1 - chan_here},
        device_id_type=MESH,
    )
    swap.start()
    for copy in late:
        copy.wait()
    offset = chan_here * half_cap
    begin = offset
    for tile in range(tiles):
        begin += jnp.where(tile < tile_here, cells_ref[tile], 0)
    cell_count = counts.shape[1]
    shift = lax.rem(2 * cell_count - begin, cell_count)

    def own(table):
        spread = jnp.broadcast_to(table.astype(jnp.float32), (8, cell_count))
        return pltpu.roll(spread, shift, 1)[0:1, :BLOCK]

    extent = own(counts[...])
    slot = lax.broadcasted_iota(jnp.int32, (1, BLOCK), 1)
    live = (slot < half_cap) & (slot + offset < cells_ref[tile_here])
    scale = jnp.where(live, 1.6 / jnp.sqrt(extent), 0.0)
    rate = own(rates[...])
    swap.wait()
    beam[...] = (
        packed[chan_here].astype(jnp.float32) + other[...].astype(jnp.float32)
    ).astype(jnp.bfloat16)
    copies = []
    for hop in range(1, tiles):
        target = lax.rem(tile_here + hop, tiles)
        copy = pltpu.make_async_remote_copy(
            src_ref=beam.at[target],
            dst_ref=columns.at[tile_here],
            send_sem=send_sems.at[hop],
            recv_sem=recv_sems.at[hop],
            device_id={"tile": target},
            device_id_type=MESH,
        )
        copy.start()
        copies.append(copy)
    columns[tile_here] = beam[tile_here]
    write_taps(extent, rate, scale, tap_ref, KMAX // 2 - pulses)
    taps = tap_ref[...]
    response = jnp.dot(spectrum[0], taps, preferred_element_type=jnp.float32) + jnp.dot(
        spectrum[1], taps, preferred_element_type=jnp.float32
    )
    for copy in copies:
        copy.wait()
    signal = columns[...].reshape(points, BLOCK)
    image = jnp.dot(forward[0], signal, preferred_element_type=jnp.float32) + jnp.dot(
        forward[1], signal, preferred_element_type=jnp.float32
    )
    real, imag = image[:points], image[points:]
    tap_real, tap_imag = response[:points], response[points:]
    product = jnp.concatenate(
        [real * tap_real - imag * tap_imag, real * tap_imag + imag * tap_real], 0
    )
    high = product.astype(jnp.bfloat16)
    low = (product - high.astype(jnp.float32)).astype(jnp.bfloat16)
    over = (((0,), (0,)), ((), ()))
    result = lax.dot_general(high, inverse[0], over, preferred_element_type=jnp.float32)
    result += lax.dot_general(low, inverse[0], over, preferred_element_type=jnp.float32)
    result += lax.dot_general(high, inverse[1], over, preferred_element_type=jnp.float32)
    out_ref[:, 0, :] = result[:slots, :pulses]
    out_ref[:, 1, :] = result[:slots, pulses:]


def focus_call(raw_echoes, range_taps, beam_weights, order, cells, counts, rates, half_cap):
    local, local_chans, _, cell_count = raw_echoes.shape
    tiles = cells.shape[0]
    pulses = tiles * local
    rows = 2 * local
    out_blocks = cell_count // BLOCK
    tables = [jnp.asarray(table) for table in fourier_tables(pulses)]
    counts, rates = counts[None], rates[None]
    arrays = [raw_echoes, range_taps, beam_weights, counts, rates] + tables
    exchanged = pltpu.VMEM((tiles, rows, BLOCK), jnp.bfloat16)
    total = pltpu.VMEM((out_blocks, rows, BLOCK), jnp.float32)
    return pl.pallas_call(
        functools.partial(focus_kernel, half_cap),
        out_shape=jax.ShapeDtypeStruct((half_cap, 2, pulses), jnp.float32),
        in_specs=[pl.BlockSpec(memory_space=pltpu.SMEM)] * 2
        + [pl.BlockSpec(memory_space=pl.ANY)] * len(arrays),
        out_specs=pl.BlockSpec(memory_space=pltpu.VMEM),
        scratch_shapes=[pltpu.VMEM((local_chans, local, 2, cell_count), raw_echoes.dtype)]
        + [pltpu.VMEM(array.shape, array.dtype) for array in arrays[1:]]
        + [
            pltpu.VMEM((out_blocks + 2, rows, BLOCK), jnp.bfloat16),
            pltpu.VMEM((BLOCK, BLOCK), jnp.bfloat16),
            total,
            total,
            pltpu.VMEM((2, tiles, rows, BLOCK), jnp.bfloat16),
            exchanged,
            exchanged,
            exchanged,
            pltpu.VMEM((4 * pulses, BLOCK), jnp.bfloat16),
            pltpu.SemaphoreType.DMA((len(arrays) - 1,)),
            pltpu.SemaphoreType.DMA((local_chans,)),
            pltpu.SemaphoreType.DMA((2,)),
            pltpu.SemaphoreType.DMA((tiles,)),
            pltpu.SemaphoreType.DMA((tiles,)),
        ],
        compiler_params=pltpu.CompilerParams(
            collective_id=0, has_side_effects=True, vmem_limit_bytes=60 << 20
        ),
    )(order, cells, *arrays)


def on_device(
    raw_echoes, range_taps, beam_weights, channel_order, group_cells, tap_counts, chirp_rates
):
    tiles = group_cells.shape[0]
    local, _, _, cell_count = raw_echoes.shape
    average = cell_count // tiles
    half_cap = (average + average // 2) // lax.axis_size("chan")
    fits = average == BLOCK and lax.axis_size("chan") == 2 and 2 * tiles * local == BLOCK
    if not fits or range_taps.shape[-1] != 2 * BLOCK:
        return generic_device(
            raw_echoes,
            range_taps,
            beam_weights,
            channel_order,
            group_cells,
            tap_counts,
            chirp_rates,
        )
    return focus_call(
        raw_echoes,
        range_taps,
        beam_weights,
        channel_order,
        group_cells,
        tap_counts,
        chirp_rates,
        half_cap,
    )


def solution(mesh):
    return jax.shard_map(
        on_device,
        mesh=mesh,
        in_specs=(P(("scene", "tile"), "chan", None, None), P(), P(), P(), P(), P(), P()),
        out_specs=P(("scene", "tile", "chan"), None, None),
        check_vma=False,
    )
```

```python
import functools

import jax
import jax.numpy as jnp
import numpy as np
from jax import lax
from jax.experimental import pallas as pl
from jax.experimental.pallas import tpu as pltpu
from jax.sharding import PartitionSpec as P

KMAX = 640


def toeplitz_rows(coeffs, block_len, span_len):
    leading = coeffs.shape[:-1]
    filler = jnp.zeros(leading + (span_len + 1 - coeffs.shape[-1],), coeffs.dtype)
    extended = jnp.concatenate([coeffs, filler], -1)
    repeated = jnp.tile(extended, (1,) * len(leading) + (block_len,))
    return repeated[..., : block_len * span_len].reshape(leading + (block_len, span_len))


def complex_matrix(toeplitz_pair):
    real_part = toeplitz_pair[..., 0, :, :]
    imag_part = toeplitz_pair[..., 1, :, :]
    from_real = jnp.stack([real_part, imag_part], -3)
    from_imag = jnp.stack([-imag_part, real_part], -3)
    return jnp.stack([from_real, from_imag], -4)


def block_windows(signal, block_len, lead_blocks, span_blocks, out_blocks):
    total_blocks = out_blocks + span_blocks - 1
    right_pad = total_blocks * block_len - lead_blocks * block_len - signal.shape[-1]
    padded = jnp.pad(signal, [(0, 0)] * (signal.ndim - 1) + [(lead_blocks * block_len, right_pad)])
    blocked = padded.reshape(signal.shape[:-1] + (total_blocks, block_len))
    return jnp.concatenate(
        [
            blocked[..., offset_block : offset_block + out_blocks, :]
            for offset_block in range(span_blocks)
        ],
        -1,
    )


def chirp_taps(counts, sweep_rates, longest):
    position = jnp.arange(longest, dtype=jnp.int32)[None, :]
    lengths = counts[:, None]
    shifted = position - (longest // 2 - lengths // 2)
    inside = (shifted >= 0) & (shifted < lengths)
    extent = lengths.astype(jnp.float32)
    located = shifted.astype(jnp.float32)
    centred = (located - 0.5 * (extent - 1.0)) / extent
    angles = jnp.pi * sweep_rates[:, None] * extent * centred * centred
    envelope = (
        (0.5 - 0.5 * jnp.cos(2.0 * jnp.pi * (located + 0.5) / extent)) * 1.6 / jnp.sqrt(extent)
    )
    envelope = jnp.where(inside, envelope, jnp.zeros_like(envelope))
    return jnp.stack([envelope * jnp.cos(angles), envelope * jnp.sin(angles)], 1)


def range_compress(echoes, filters):
    block_len = filters.shape[-1] // 2
    windows = block_windows(echoes, block_len, 1, 3, echoes.shape[-1] // block_len)
    matrices = complex_matrix(toeplitz_rows(filters, block_len, 3 * block_len))
    product = jnp.einsum(
        "pcanw,caeiw->pceni", windows, matrices, preferred_element_type=jnp.float32
    )
    return product.reshape(echoes.shape)


def azimuth_focus(columns, coeffs):
    block_len = coeffs.shape[-1] // 8
    pulses = columns.shape[-1]
    out_blocks = -(-pulses // block_len)
    windows = block_windows(columns, block_len, 4, 9, out_blocks)
    matrices = complex_matrix(toeplitz_rows(coeffs, block_len, 9 * block_len))
    product = jnp.einsum("sanw,saeiw->seni", windows, matrices, preferred_element_type=jnp.float32)
    return product.reshape(columns.shape[:-1] + (out_blocks * block_len,))[..., :pulses]


def owner_slots(signal, group_starts, group_sizes, offset, slot_width, margin):
    padded = jnp.pad(signal, [(0, 0)] * (signal.ndim - 1) + [(0, margin)])

    def one_group(start_cell, size_cells):
        window_cut = lax.dynamic_slice_in_dim(
            padded, start_cell + offset, slot_width, signal.ndim - 1
        )
        inside = jnp.arange(slot_width, dtype=jnp.int32) + offset < size_cells
        return jnp.where(inside, window_cut, jnp.zeros_like(window_cut))

    return jax.vmap(one_group)(group_starts, group_sizes)


def generic_device(
    raw_echoes, range_taps, beam_weights, channel_order, group_cells, tap_counts, chirp_rates
):
    local_chans = raw_echoes.shape[1]
    all_chans = range_taps.shape[0]
    first_slot = lax.axis_index("chan") * local_chans
    own_channels = lax.dynamic_slice_in_dim(channel_order, first_slot, local_chans)
    selector = (own_channels[:, None] == jnp.arange(all_chans, dtype=jnp.int32)[None, :]).astype(
        jnp.bfloat16
    )
    filters = jnp.dot(
        selector, range_taps.reshape(all_chans, -1), preferred_element_type=jnp.float32
    )
    filters = filters.astype(jnp.bfloat16).reshape(local_chans, 2, -1)
    weights = jnp.dot(
        selector, beam_weights.reshape(all_chans, -1), preferred_element_type=jnp.float32
    )
    weights = weights.reshape(local_chans, 2, -1)
    spectra = range_compress(raw_echoes, filters)
    real_sum = jnp.sum(spectra[:, :, 0] * weights[:, 0] - spectra[:, :, 1] * weights[:, 1], 1)
    imag_sum = jnp.sum(spectra[:, :, 0] * weights[:, 1] + spectra[:, :, 1] * weights[:, 0], 1)
    partial_value = jnp.stack([real_sum, imag_sum], 1)
    tile_count = group_cells.shape[0]
    cell_count = raw_echoes.shape[-1]
    average = cell_count // tile_count
    capacity = average + average // 2
    chan_ways = lax.axis_size("chan")
    half_cap = capacity // chan_ways
    group_starts = jnp.cumsum(group_cells) - group_cells
    chan_offset = lax.axis_index("chan") * half_cap
    summed = lax.psum(partial_value.astype(jnp.bfloat16), "chan")
    outgoing = owner_slots(summed, group_starts, group_cells, chan_offset, half_cap, capacity)
    outgoing = outgoing.transpose(0, 3, 2, 1)
    incoming = lax.all_to_all(outgoing, "tile", split_axis=0, concat_axis=3, tiled=True)
    columns = incoming[0]
    tile_here = lax.axis_index("tile")
    begin_cell = lax.dynamic_index_in_dim(group_starts, tile_here, keepdims=False)
    owned_cells = lax.dynamic_index_in_dim(group_cells, tile_here, keepdims=False)
    local_slot = chan_offset + jnp.arange(half_cap, dtype=jnp.int32)
    inside = local_slot < owned_cells
    count_table = jnp.pad(tap_counts, (0, capacity), mode="edge")
    rate_table = jnp.pad(chirp_rates, (0, capacity), mode="edge")
    count_here = lax.dynamic_slice_in_dim(count_table, begin_cell + chan_offset, half_cap)
    rate_here = lax.dynamic_slice_in_dim(rate_table, begin_cell + chan_offset, half_cap)
    taps_here = chirp_taps(count_here, rate_here, KMAX)
    taps_here = jnp.where(inside[:, None, None], taps_here, jnp.zeros_like(taps_here)).astype(
        jnp.bfloat16
    )
    return azimuth_focus(columns, taps_here)


MESH = pl.DeviceIdType.MESH
BLOCK = 256
SPAN = 3 * BLOCK


def split_bf16(matrix):
    high = matrix.astype(jnp.bfloat16)
    low = (matrix - high.astype(np.float64)).astype(jnp.bfloat16)
    return np.stack([high, low])


def fourier_tables(pulses):
    points = 2 * pulses
    freq = np.arange(points)[:, None]
    unit = 2.0 * np.pi / points

    def rotation(index, sign):
        angle = unit * ((freq * index[None, :]) % points)
        return np.cos(angle), sign * np.sin(angle)

    cos_x, sin_x = rotation(np.arange(pulses), -1.0)
    forward = np.block([[cos_x, -sin_x], [sin_x, cos_x]])
    order = np.arange(2 * pulses).reshape(2, pulses).T.reshape(-1)
    forward = forward[:, order]
    cos_h, sin_h = rotation(pulses - np.arange(points), -1.0)
    taps = np.block([[cos_h, -sin_h], [sin_h, cos_h]])
    cos_y, sin_y = rotation(np.arange(pulses), 1.0)
    inverse = np.block([[cos_y, sin_y], [-sin_y, cos_y]]) / points
    return split_bf16(forward), split_bf16(taps), split_bf16(inverse)


def even_series(square, terms):
    value = jnp.full_like(square, terms[-1])
    for term in reversed(terms[:-1]):
        value = value * square + term
    return value


COS_TERMS = [(-1.0) ** n * (2 * np.pi) ** (2 * n) / float(np.prod(np.arange(1, 2 * n + 1, dtype=np.float64))) for n in range(9)]
SIN_TERMS = [(-1.0) ** n * (2 * np.pi) ** (2 * n + 1) / float(np.prod(np.arange(1, 2 * n + 2, dtype=np.float64))) for n in range(9)]


def write_taps(extent, rate, scale, tap_ref, first_tap):
    rows = tap_ref.shape[0] // 2
    length = extent.astype(jnp.int32)
    start = KMAX // 2 - length // 2
    inverse = 1.0 / extent
    turn = 0.5 * rate * extent
    for at in range(0, rows, 32):
        tap = lax.broadcasted_iota(jnp.int32, (32, BLOCK), 0) + (first_tap + at)
        shifted = tap - start
        inside = (shifted >= 0) & (shifted < length)
        centred = (shifted.astype(jnp.float32) - 0.5 * (extent - 1.0)) * inverse
        square = centred * centred
        envelope = jnp.where(inside, scale * (0.5 + 0.5 * even_series(square, COS_TERMS)), 0.0)
        turns = turn * square
        turns = turns - jnp.floor(turns + 0.5)
        turn_square = turns * turns
        real = envelope * even_series(turn_square, COS_TERMS)
        imag = envelope * (turns * even_series(turn_square, SIN_TERMS))
        tap_ref[at : at + 32] = real.astype(jnp.bfloat16)
        tap_ref[rows + at : rows + at + 32] = imag.astype(jnp.bfloat16)


def focus_kernel(
    half_cap,
    order_ref,
    cells_ref,
    raw_ref,
    filter_ref,
    weight_ref,
    count_ref,
    rate_ref,
    forward_ref,
    spectrum_ref,
    inverse_ref,
    out_ref,
    raw,
    filters,
    weights,
    counts,
    rates,
    forward,
    spectrum,
    inverse,
    blocks,
    mirror,
    straight,
    crossed,
    packed,
    other,
    beam,
    columns,
    tap_ref,
    load_sems,
    raw_sems,
    pair_sems,
    send_sems,
    recv_sems,
):
    tiles = beam.shape[0]
    tile_here = lax.axis_index("tile")
    chan_here = lax.axis_index("chan")
    local_chans = raw.shape[0]
    out_blocks = blocks.shape[0] - 2
    rows = blocks.shape[1]
    slots, _, pulses = out_ref.shape
    points = 2 * pulses
    barrier = pltpu.get_barrier_semaphore()
    pl.semaphore_signal(barrier, inc=1, device_id={"chan": 1 - chan_here}, device_id_type=MESH)
    for hop in range(1, tiles):
        target = lax.rem(tile_here + hop, tiles)
        pl.semaphore_signal(barrier, inc=1, device_id={"tile": target}, device_id_type=MESH)

    def fetch(source, target, at):
        return pltpu.make_async_copy(source, target, load_sems.at[at])

    def fetch_raw(chan):
        return pltpu.make_async_copy(raw_ref.at[:, chan], raw.at[chan], raw_sems.at[chan])

    get_filters = fetch(filter_ref, filters, 0)
    get_weights = fetch(weight_ref, weights, 1)
    late = [
        fetch(count_ref, counts, 2),
        fetch(rate_ref, rates, 3),
        fetch(spectrum_ref, spectrum, 4),
        fetch(forward_ref, forward, 5),
        fetch(inverse_ref, inverse, 6),
    ]
    get_filters.start()
    get_weights.start()
    for chan in range(local_chans):
        fetch_raw(chan).start()
    for copy in late:
        copy.start()

    edge = jnp.zeros((rows, BLOCK), jnp.bfloat16)
    blocks[0] = edge
    blocks[out_blocks + 1] = edge
    straight[...] = jnp.zeros_like(straight)
    crossed[...] = jnp.zeros_like(crossed)
    row = lax.broadcasted_iota(jnp.int32, (BLOCK, BLOCK), 0)
    lane = lax.broadcasted_iota(jnp.int32, (BLOCK, BLOCK), 1)
    mirror[...] = jnp.where(row + lane == BLOCK - 1, 1.0, 0.0).astype(jnp.bfloat16)
    get_filters.wait()
    get_weights.wait()

    def one_channel(chan, carry):
        physical = order_ref[chan_here * local_chans + chan]
        own_filter = filters[physical]
        own_weight = weights[physical].astype(jnp.float32)
        fetch_raw(chan).wait()
        for block in range(out_blocks):
            cells = slice(block * BLOCK, (block + 1) * BLOCK)
            blocks[block + 1] = raw[chan, :, :, cells].reshape(rows, BLOCK)

        first_half = jnp.dot(
            own_filter[:, :BLOCK], mirror[...], preferred_element_type=jnp.float32
        )
        second_half = jnp.dot(
            own_filter[:, BLOCK:], mirror[...], preferred_element_type=jnp.float32
        )
        backward = jnp.concatenate([jnp.zeros_like(first_half), second_half, first_half], 1)

        def toeplitz(part):
            row = jnp.broadcast_to(backward[part : part + 1], (128, SPAN))
            top = pltpu.roll(row, 1, 1, stride=1, stride_axis=0).astype(jnp.bfloat16)
            low = jnp.concatenate([top[:, SPAN - 128 :], top[:, : SPAN - 128]], 1)
            return jnp.concatenate([top, low], 0)

        real_rows = toeplitz(0)
        imag_rows = toeplitz(1)
        total = None
        for step in range(3):
            at = (SPAN - BLOCK * step) % SPAN
            matrix = jnp.concatenate(
                [real_rows[:, at : at + BLOCK], imag_rows[:, at : at + BLOCK]], 1
            )
            window = blocks[step : step + out_blocks].reshape(out_blocks * rows, BLOCK)
            term = jnp.dot(window, matrix, preferred_element_type=jnp.float32)
            total = term if total is None else total + term
        for block in range(out_blocks):
            cells = slice(block * BLOCK, (block + 1) * BLOCK)
            weight_real = own_weight[0:1, cells]
            weight_imag = own_weight[1:2, cells]
            by_real = total[block * rows : (block + 1) * rows, :BLOCK]
            by_imag = total[block * rows : (block + 1) * rows, BLOCK:]
            straight[block] += weight_real * by_real - weight_imag * by_imag
            crossed[block] += weight_imag * by_real + weight_real * by_imag
        return carry

    lax.fori_loop(0, local_chans, one_channel, 0)

    width = 2 * BLOCK
    is_real = lax.broadcasted_iota(jnp.int32, (rows, BLOCK), 0) % 2 == 0

    def summed(block):
        turned = crossed[block]
        return straight[block] + jnp.where(
            is_real, -pltpu.roll(turned, rows - 1, 0), pltpu.roll(turned, 1, 0)
        )

    is_left = lax.broadcasted_iota(jnp.int32, (rows // 2, 128), 1) < 64

    def pack(chan, tile, values):
        last = values[:, 128:BLOCK]
        folded = jnp.where(is_left, last[: rows // 2], pltpu.roll(last[rows // 2 :], 64, 1))
        packed[chan, tile, :rows] = values[:, :128].astype(jnp.bfloat16)
        packed[chan, tile, rows:] = folded.astype(jnp.bfloat16)

    def unpack(block):
        folded = block[rows:]
        turned = pltpu.roll(folded.astype(jnp.float32), 64, 1).astype(jnp.bfloat16)
        return jnp.concatenate([block[:rows], jnp.concatenate([folded, turned], 0)], 1)

    for pair in range(out_blocks // 2):
        first = cells_ref[2 * pair]
        values = jnp.concatenate([summed(2 * pair), summed(2 * pair + 1)], 1)
        moved = pltpu.roll(values, width - first, 1)
        pack(0, 2 * pair, values)
        pack(0, 2 * pair + 1, moved)
        values = pltpu.roll(values, width - half_cap, 1)
        moved = pltpu.roll(moved, width - half_cap, 1)
        pack(1, 2 * pair, values)
        pack(1, 2 * pair + 1, moved)

    pl.semaphore_wait(barrier, tiles)
    swap = pltpu.make_async_remote_copy(
        src_ref=packed.at[1 - chan_here],
        dst_ref=other,
        send_sem=pair_sems.at[0],
        recv_sem=pair_sems.at[1],
        device_id={"chan": 1 - chan_here},
        device_id_type=MESH,
    )
    swap.start()
    for copy in late:
        copy.wait()
    offset = chan_here * half_cap
    begin = offset
    for tile in range(tiles):
        begin += jnp.where(tile < tile_here, cells_ref[tile], 0)
    cell_count = counts.shape[1]
    shift = lax.rem(2 * cell_count - begin, cell_count)

    def own(table):
        spread = jnp.broadcast_to(table.astype(jnp.float32), (8, cell_count))
        return pltpu.roll(spread, shift, 1)[0:1, :BLOCK]

    extent = own(counts[...])
    slot = lax.broadcasted_iota(jnp.int32, (1, BLOCK), 1)
    live = (slot < half_cap) & (slot + offset < cells_ref[tile_here])
    scale = jnp.where(live, 1.6 / jnp.sqrt(extent), 0.0)
    rate = own(rates[...])
    swap.wait()
    beam[...] = (
        packed[chan_here].astype(jnp.float32) + other[...].astype(jnp.float32)
    ).astype(jnp.bfloat16)
    copies = []
    for hop in range(1, tiles):
        target = lax.rem(tile_here + hop, tiles)
        copy = pltpu.make_async_remote_copy(
            src_ref=beam.at[target],
            dst_ref=columns.at[tile_here],
            send_sem=send_sems.at[hop],
            recv_sem=recv_sems.at[hop],
            device_id={"tile": target},
            device_id_type=MESH,
        )
        copy.start()
        copies.append(copy)
    columns[tile_here] = beam[tile_here]
    write_taps(extent, rate, scale, tap_ref, KMAX // 2 - pulses)
    taps = tap_ref[...]
    response = jnp.dot(spectrum[0], taps, preferred_element_type=jnp.float32) + jnp.dot(
        spectrum[1], taps, preferred_element_type=jnp.float32
    )
    for copy in copies:
        copy.wait()
    signal = jnp.concatenate([unpack(columns[tile]) for tile in range(tiles)], 0)
    image = jnp.dot(forward[0], signal, preferred_element_type=jnp.float32) + jnp.dot(
        forward[1], signal, preferred_element_type=jnp.float32
    )
    real, imag = image[:points], image[points:]
    tap_real, tap_imag = response[:points], response[points:]
    product = jnp.concatenate(
        [real * tap_real - imag * tap_imag, real * tap_imag + imag * tap_real], 0
    )
    high = product.astype(jnp.bfloat16)
    low = (product - high.astype(jnp.float32)).astype(jnp.bfloat16)
    over = (((0,), (0,)), ((), ()))
    result = lax.dot_general(high, inverse[0], over, preferred_element_type=jnp.float32)
    result += lax.dot_general(low, inverse[0], over, preferred_element_type=jnp.float32)
    result += lax.dot_general(high, inverse[1], over, preferred_element_type=jnp.float32)
    out_ref[:, 0, :] = result[:slots, :pulses]
    out_ref[:, 1, :] = result[:slots, pulses:]


def focus_call(raw_echoes, range_taps, beam_weights, order, cells, counts, rates, half_cap):
    local, local_chans, _, cell_count = raw_echoes.shape
    tiles = cells.shape[0]
    pulses = tiles * local
    rows = 2 * local
    out_blocks = cell_count // BLOCK
    tables = [jnp.asarray(table) for table in fourier_tables(pulses)]
    counts, rates = counts[None], rates[None]
    arrays = [raw_echoes, range_taps, beam_weights, counts, rates] + tables
    exchanged = pltpu.VMEM((tiles, 3 * rows // 2, 128), jnp.bfloat16)
    total = pltpu.VMEM((out_blocks, rows, BLOCK), jnp.float32)
    return pl.pallas_call(
        functools.partial(focus_kernel, half_cap),
        out_shape=pltpu.VMEM((half_cap, 2, pulses), jnp.float32),
        in_specs=[pl.BlockSpec(memory_space=pltpu.SMEM)] * 2
        + [pl.BlockSpec(memory_space=pl.ANY)] * len(arrays),
        out_specs=pl.BlockSpec(memory_space=pltpu.VMEM),
        scratch_shapes=[pltpu.VMEM((local_chans, local, 2, cell_count), raw_echoes.dtype)]
        + [pltpu.VMEM(array.shape, array.dtype) for array in arrays[1:]]
        + [
            pltpu.VMEM((out_blocks + 2, rows, BLOCK), jnp.bfloat16),
            pltpu.VMEM((BLOCK, BLOCK), jnp.bfloat16),
            total,
            total,
            pltpu.VMEM((2, tiles, 3 * rows // 2, 128), jnp.bfloat16),
            exchanged,
            exchanged,
            exchanged,
            pltpu.VMEM((4 * pulses, BLOCK), jnp.bfloat16),
            pltpu.SemaphoreType.DMA((len(arrays) - 1,)),
            pltpu.SemaphoreType.DMA((local_chans,)),
            pltpu.SemaphoreType.DMA((2,)),
            pltpu.SemaphoreType.DMA((tiles,)),
            pltpu.SemaphoreType.DMA((tiles,)),
        ],
        compiler_params=pltpu.CompilerParams(
            collective_id=0, has_side_effects=True, vmem_limit_bytes=56 << 20
        ),
    )(order, cells, *arrays)


def on_device(
    raw_echoes, range_taps, beam_weights, channel_order, group_cells, tap_counts, chirp_rates
):
    tiles = group_cells.shape[0]
    local, _, _, cell_count = raw_echoes.shape
    average = cell_count // tiles
    half_cap = (average + average // 2) // lax.axis_size("chan")
    fits = average == BLOCK and lax.axis_size("chan") == 2 and 2 * tiles * local == BLOCK
    if not fits or range_taps.shape[-1] != 2 * BLOCK:
        return generic_device(
            raw_echoes,
            range_taps,
            beam_weights,
            channel_order,
            group_cells,
            tap_counts,
            chirp_rates,
        )
    return focus_call(
        raw_echoes,
        range_taps,
        beam_weights,
        channel_order,
        group_cells,
        tap_counts,
        chirp_rates,
        half_cap,
    )


def solution(mesh):
    return jax.shard_map(
        on_device,
        mesh=mesh,
        in_specs=(P(("scene", "tile"), "chan", None, None), P(), P(), P(), P(), P(), P()),
        out_specs=P(("scene", "tile", "chan"), None, None),
        check_vma=False,
    )
```

```python
import functools

import jax
import jax.numpy as jnp
import numpy as np
from jax import lax
from jax.experimental import pallas as pl
from jax.experimental.pallas import tpu as pltpu
from jax.sharding import PartitionSpec as P

KMAX = 640


def toeplitz_rows(coeffs, block_len, span_len):
    leading = coeffs.shape[:-1]
    filler = jnp.zeros(leading + (span_len + 1 - coeffs.shape[-1],), coeffs.dtype)
    extended = jnp.concatenate([coeffs, filler], -1)
    repeated = jnp.tile(extended, (1,) * len(leading) + (block_len,))
    return repeated[..., : block_len * span_len].reshape(leading + (block_len, span_len))


def complex_matrix(toeplitz_pair):
    real_part = toeplitz_pair[..., 0, :, :]
    imag_part = toeplitz_pair[..., 1, :, :]
    from_real = jnp.stack([real_part, imag_part], -3)
    from_imag = jnp.stack([-imag_part, real_part], -3)
    return jnp.stack([from_real, from_imag], -4)


def block_windows(signal, block_len, lead_blocks, span_blocks, out_blocks):
    total_blocks = out_blocks + span_blocks - 1
    right_pad = total_blocks * block_len - lead_blocks * block_len - signal.shape[-1]
    padded = jnp.pad(signal, [(0, 0)] * (signal.ndim - 1) + [(lead_blocks * block_len, right_pad)])
    blocked = padded.reshape(signal.shape[:-1] + (total_blocks, block_len))
    return jnp.concatenate(
        [
            blocked[..., offset_block : offset_block + out_blocks, :]
            for offset_block in range(span_blocks)
        ],
        -1,
    )


def chirp_taps(counts, sweep_rates, longest):
    position = jnp.arange(longest, dtype=jnp.int32)[None, :]
    lengths = counts[:, None]
    shifted = position - (longest // 2 - lengths // 2)
    inside = (shifted >= 0) & (shifted < lengths)
    extent = lengths.astype(jnp.float32)
    located = shifted.astype(jnp.float32)
    centred = (located - 0.5 * (extent - 1.0)) / extent
    angles = jnp.pi * sweep_rates[:, None] * extent * centred * centred
    envelope = (
        (0.5 - 0.5 * jnp.cos(2.0 * jnp.pi * (located + 0.5) / extent)) * 1.6 / jnp.sqrt(extent)
    )
    envelope = jnp.where(inside, envelope, jnp.zeros_like(envelope))
    return jnp.stack([envelope * jnp.cos(angles), envelope * jnp.sin(angles)], 1)


def range_compress(echoes, filters):
    block_len = filters.shape[-1] // 2
    windows = block_windows(echoes, block_len, 1, 3, echoes.shape[-1] // block_len)
    matrices = complex_matrix(toeplitz_rows(filters, block_len, 3 * block_len))
    product = jnp.einsum(
        "pcanw,caeiw->pceni", windows, matrices, preferred_element_type=jnp.float32
    )
    return product.reshape(echoes.shape)


def azimuth_focus(columns, coeffs):
    block_len = coeffs.shape[-1] // 8
    pulses = columns.shape[-1]
    out_blocks = -(-pulses // block_len)
    windows = block_windows(columns, block_len, 4, 9, out_blocks)
    matrices = complex_matrix(toeplitz_rows(coeffs, block_len, 9 * block_len))
    product = jnp.einsum("sanw,saeiw->seni", windows, matrices, preferred_element_type=jnp.float32)
    return product.reshape(columns.shape[:-1] + (out_blocks * block_len,))[..., :pulses]


def owner_slots(signal, group_starts, group_sizes, offset, slot_width, margin):
    padded = jnp.pad(signal, [(0, 0)] * (signal.ndim - 1) + [(0, margin)])

    def one_group(start_cell, size_cells):
        window_cut = lax.dynamic_slice_in_dim(
            padded, start_cell + offset, slot_width, signal.ndim - 1
        )
        inside = jnp.arange(slot_width, dtype=jnp.int32) + offset < size_cells
        return jnp.where(inside, window_cut, jnp.zeros_like(window_cut))

    return jax.vmap(one_group)(group_starts, group_sizes)


def generic_device(
    raw_echoes, range_taps, beam_weights, channel_order, group_cells, tap_counts, chirp_rates
):
    local_chans = raw_echoes.shape[1]
    all_chans = range_taps.shape[0]
    first_slot = lax.axis_index("chan") * local_chans
    own_channels = lax.dynamic_slice_in_dim(channel_order, first_slot, local_chans)
    selector = (own_channels[:, None] == jnp.arange(all_chans, dtype=jnp.int32)[None, :]).astype(
        jnp.bfloat16
    )
    filters = jnp.dot(
        selector, range_taps.reshape(all_chans, -1), preferred_element_type=jnp.float32
    )
    filters = filters.astype(jnp.bfloat16).reshape(local_chans, 2, -1)
    weights = jnp.dot(
        selector, beam_weights.reshape(all_chans, -1), preferred_element_type=jnp.float32
    )
    weights = weights.reshape(local_chans, 2, -1)
    spectra = range_compress(raw_echoes, filters)
    real_sum = jnp.sum(spectra[:, :, 0] * weights[:, 0] - spectra[:, :, 1] * weights[:, 1], 1)
    imag_sum = jnp.sum(spectra[:, :, 0] * weights[:, 1] + spectra[:, :, 1] * weights[:, 0], 1)
    partial_value = jnp.stack([real_sum, imag_sum], 1)
    tile_count = group_cells.shape[0]
    cell_count = raw_echoes.shape[-1]
    average = cell_count // tile_count
    capacity = average + average // 2
    chan_ways = lax.axis_size("chan")
    half_cap = capacity // chan_ways
    group_starts = jnp.cumsum(group_cells) - group_cells
    chan_offset = lax.axis_index("chan") * half_cap
    summed = lax.psum(partial_value.astype(jnp.bfloat16), "chan")
    outgoing = owner_slots(summed, group_starts, group_cells, chan_offset, half_cap, capacity)
    outgoing = outgoing.transpose(0, 3, 2, 1)
    incoming = lax.all_to_all(outgoing, "tile", split_axis=0, concat_axis=3, tiled=True)
    columns = incoming[0]
    tile_here = lax.axis_index("tile")
    begin_cell = lax.dynamic_index_in_dim(group_starts, tile_here, keepdims=False)
    owned_cells = lax.dynamic_index_in_dim(group_cells, tile_here, keepdims=False)
    local_slot = chan_offset + jnp.arange(half_cap, dtype=jnp.int32)
    inside = local_slot < owned_cells
    count_table = jnp.pad(tap_counts, (0, capacity), mode="edge")
    rate_table = jnp.pad(chirp_rates, (0, capacity), mode="edge")
    count_here = lax.dynamic_slice_in_dim(count_table, begin_cell + chan_offset, half_cap)
    rate_here = lax.dynamic_slice_in_dim(rate_table, begin_cell + chan_offset, half_cap)
    taps_here = chirp_taps(count_here, rate_here, KMAX)
    taps_here = jnp.where(inside[:, None, None], taps_here, jnp.zeros_like(taps_here)).astype(
        jnp.bfloat16
    )
    return azimuth_focus(columns, taps_here)


MESH = pl.DeviceIdType.MESH
BLOCK = 256
SPAN = 3 * BLOCK


def split_bf16(matrix):
    high = matrix.astype(jnp.bfloat16)
    low = (matrix - high.astype(np.float64)).astype(jnp.bfloat16)
    return np.stack([high, low])


def fourier_tables(pulses):
    points = 2 * pulses
    freq = np.arange(points)[:, None]
    unit = 2.0 * np.pi / points

    def rotation(index, sign):
        angle = unit * ((freq * index[None, :]) % points)
        return np.cos(angle), sign * np.sin(angle)

    cos_x, sin_x = rotation(np.arange(pulses), -1.0)
    forward = np.block([[cos_x, -sin_x], [sin_x, cos_x]])
    order = np.arange(2 * pulses).reshape(2, pulses).T.reshape(-1)
    forward = forward[:, order]
    cos_h, sin_h = rotation(pulses - np.arange(points), -1.0)
    taps = np.block([[cos_h, -sin_h], [sin_h, cos_h]])
    cos_y, sin_y = rotation(np.arange(pulses), 1.0)
    inverse = np.block([[cos_y, sin_y], [-sin_y, cos_y]]) / points
    return split_bf16(forward), split_bf16(taps), split_bf16(inverse)


def even_series(square, terms):
    value = jnp.full_like(square, terms[-1])
    for term in reversed(terms[:-1]):
        value = value * square + term
    return value


COS_TERMS = [(-1.0) ** n * (2 * np.pi) ** (2 * n) / float(np.prod(np.arange(1, 2 * n + 1, dtype=np.float64))) for n in range(9)]
SIN_TERMS = [(-1.0) ** n * (2 * np.pi) ** (2 * n + 1) / float(np.prod(np.arange(1, 2 * n + 2, dtype=np.float64))) for n in range(9)]


def write_taps(extent, rate, scale, tap_ref, first_tap):
    rows = tap_ref.shape[0] // 2
    length = extent.astype(jnp.int32)
    start = KMAX // 2 - length // 2
    inverse = 1.0 / extent
    turn = 0.5 * rate * extent
    for at in range(0, rows, 32):
        tap = lax.broadcasted_iota(jnp.int32, (32, BLOCK), 0) + (first_tap + at)
        shifted = tap - start
        inside = (shifted >= 0) & (shifted < length)
        centred = (shifted.astype(jnp.float32) - 0.5 * (extent - 1.0)) * inverse
        square = centred * centred
        envelope = jnp.where(inside, scale * (0.5 + 0.5 * even_series(square, COS_TERMS)), 0.0)
        turns = turn * square
        turns = turns - jnp.floor(turns + 0.5)
        turn_square = turns * turns
        real = envelope * even_series(turn_square, COS_TERMS)
        imag = envelope * (turns * even_series(turn_square, SIN_TERMS))
        tap_ref[at : at + 32] = real.astype(jnp.bfloat16)
        tap_ref[rows + at : rows + at + 32] = imag.astype(jnp.bfloat16)


def focus_kernel(
    half_cap,
    order_hbm,
    cells_hbm,
    raw_ref,
    filter_ref,
    weight_ref,
    count_ref,
    rate_ref,
    forward_ref,
    spectrum_ref,
    inverse_ref,
    out_ref,
    order_ref,
    cells_ref,
    raw,
    filters,
    weights,
    counts,
    rates,
    forward,
    spectrum,
    inverse,
    blocks,
    mirror,
    straight,
    crossed,
    packed,
    other,
    beam,
    columns,
    tap_ref,
    load_sems,
    raw_sems,
    pair_sems,
    send_sems,
    recv_sems,
):
    tiles = beam.shape[0]
    tile_here = lax.axis_index("tile")
    chan_here = lax.axis_index("chan")
    local_chans = raw.shape[0]
    out_blocks = blocks.shape[0] - 2
    rows = blocks.shape[1]
    slots, _, pulses = out_ref.shape
    points = 2 * pulses
    barrier = pltpu.get_barrier_semaphore()
    pl.semaphore_signal(barrier, inc=1, device_id={"chan": 1 - chan_here}, device_id_type=MESH)
    for hop in range(1, tiles):
        target = lax.rem(tile_here + hop, tiles)
        pl.semaphore_signal(barrier, inc=1, device_id={"tile": target}, device_id_type=MESH)

    def fetch(source, target, at):
        return pltpu.make_async_copy(source, target, load_sems.at[at])

    def fetch_raw(chan):
        return pltpu.make_async_copy(raw_ref.at[:, chan], raw.at[chan], raw_sems.at[chan])

    get_filters = fetch(filter_ref, filters, 0)
    get_weights = fetch(weight_ref, weights, 1)
    late = [
        fetch(count_ref, counts, 2),
        fetch(rate_ref, rates, 3),
        fetch(spectrum_ref, spectrum, 4),
        fetch(forward_ref, forward, 5),
        fetch(inverse_ref, inverse, 6),
    ]
    get_order = fetch(order_hbm, order_ref, 7)
    get_cells = fetch(cells_hbm, cells_ref, 8)
    get_order.start()
    get_cells.start()
    get_filters.start()
    get_weights.start()
    for chan in range(local_chans):
        fetch_raw(chan).start()
    for copy in late:
        copy.start()

    edge = jnp.zeros((rows, BLOCK), jnp.bfloat16)
    blocks[0] = edge
    blocks[out_blocks + 1] = edge
    straight[...] = jnp.zeros_like(straight)
    crossed[...] = jnp.zeros_like(crossed)
    row = lax.broadcasted_iota(jnp.int32, (BLOCK, BLOCK), 0)
    lane = lax.broadcasted_iota(jnp.int32, (BLOCK, BLOCK), 1)
    mirror[...] = jnp.where(row + lane == BLOCK - 1, 1.0, 0.0).astype(jnp.bfloat16)
    get_order.wait()
    get_cells.wait()
    get_filters.wait()
    get_weights.wait()

    def one_channel(chan, carry):
        physical = order_ref[chan_here * local_chans + chan]
        own_filter = filters[physical]
        own_weight = weights[physical].astype(jnp.float32)
        fetch_raw(chan).wait()
        for block in range(out_blocks):
            cells = slice(block * BLOCK, (block + 1) * BLOCK)
            blocks[block + 1] = raw[chan, :, :, cells].reshape(rows, BLOCK)

        first_half = jnp.dot(
            own_filter[:, :BLOCK], mirror[...], preferred_element_type=jnp.float32
        )
        second_half = jnp.dot(
            own_filter[:, BLOCK:], mirror[...], preferred_element_type=jnp.float32
        )
        backward = jnp.concatenate([jnp.zeros_like(first_half), second_half, first_half], 1)

        def toeplitz(part):
            row = jnp.broadcast_to(backward[part : part + 1], (128, SPAN))
            top = pltpu.roll(row, 1, 1, stride=1, stride_axis=0).astype(jnp.bfloat16)
            low = jnp.concatenate([top[:, SPAN - 128 :], top[:, : SPAN - 128]], 1)
            return jnp.concatenate([top, low], 0)

        real_rows = toeplitz(0)
        imag_rows = toeplitz(1)
        total = None
        for step in range(3):
            at = (SPAN - BLOCK * step) % SPAN
            matrix = jnp.concatenate(
                [real_rows[:, at : at + BLOCK], imag_rows[:, at : at + BLOCK]], 1
            )
            window = blocks[step : step + out_blocks].reshape(out_blocks * rows, BLOCK)
            term = jnp.dot(window, matrix, preferred_element_type=jnp.float32)
            total = term if total is None else total + term
        for block in range(out_blocks):
            cells = slice(block * BLOCK, (block + 1) * BLOCK)
            weight_real = own_weight[0:1, cells]
            weight_imag = own_weight[1:2, cells]
            by_real = total[block * rows : (block + 1) * rows, :BLOCK]
            by_imag = total[block * rows : (block + 1) * rows, BLOCK:]
            straight[block] += weight_real * by_real - weight_imag * by_imag
            crossed[block] += weight_imag * by_real + weight_real * by_imag
        return carry

    lax.fori_loop(0, local_chans, one_channel, 0)

    width = 2 * BLOCK
    is_real = lax.broadcasted_iota(jnp.int32, (rows, BLOCK), 0) % 2 == 0

    def summed(block):
        turned = crossed[block]
        return straight[block] + jnp.where(
            is_real, -pltpu.roll(turned, rows - 1, 0), pltpu.roll(turned, 1, 0)
        )

    is_left = lax.broadcasted_iota(jnp.int32, (rows // 2, 128), 1) < 64

    def pack(chan, tile, values):
        last = values[:, 128:BLOCK]
        folded = jnp.where(is_left, last[: rows // 2], pltpu.roll(last[rows // 2 :], 64, 1))
        packed[chan, tile, :rows] = values[:, :128].astype(jnp.bfloat16)
        packed[chan, tile, rows:] = folded.astype(jnp.bfloat16)

    def unpack(block):
        folded = block[rows:]
        turned = pltpu.roll(folded.astype(jnp.float32), 64, 1).astype(jnp.bfloat16)
        return jnp.concatenate([block[:rows], jnp.concatenate([folded, turned], 0)], 1)

    for pair in range(out_blocks // 2):
        first = cells_ref[2 * pair]
        values = jnp.concatenate([summed(2 * pair), summed(2 * pair + 1)], 1)
        moved = pltpu.roll(values, width - first, 1)
        pack(0, 2 * pair, values)
        pack(0, 2 * pair + 1, moved)
        values = pltpu.roll(values, width - half_cap, 1)
        moved = pltpu.roll(moved, width - half_cap, 1)
        pack(1, 2 * pair, values)
        pack(1, 2 * pair + 1, moved)

    pl.semaphore_wait(barrier, tiles)
    swap = pltpu.make_async_remote_copy(
        src_ref=packed.at[1 - chan_here],
        dst_ref=other,
        send_sem=pair_sems.at[0],
        recv_sem=pair_sems.at[1],
        device_id={"chan": 1 - chan_here},
        device_id_type=MESH,
    )
    swap.start()
    for copy in late:
        copy.wait()
    offset = chan_here * half_cap
    begin = offset
    for tile in range(tiles):
        begin += jnp.where(tile < tile_here, cells_ref[tile], 0)
    cell_count = counts.shape[1]
    shift = lax.rem(2 * cell_count - begin, cell_count)

    def own(table):
        spread = jnp.broadcast_to(table.astype(jnp.float32), (8, cell_count))
        return pltpu.roll(spread, shift, 1)[0:1, :BLOCK]

    extent = own(counts[...])
    slot = lax.broadcasted_iota(jnp.int32, (1, BLOCK), 1)
    live = (slot < half_cap) & (slot + offset < cells_ref[tile_here])
    scale = jnp.where(live, 1.6 / jnp.sqrt(extent), 0.0)
    rate = own(rates[...])
    swap.wait()
    beam[...] = (
        packed[chan_here].astype(jnp.float32) + other[...].astype(jnp.float32)
    ).astype(jnp.bfloat16)
    copies = []
    for hop in range(1, tiles):
        target = lax.rem(tile_here + hop, tiles)
        copy = pltpu.make_async_remote_copy(
            src_ref=beam.at[target],
            dst_ref=columns.at[tile_here],
            send_sem=send_sems.at[hop],
            recv_sem=recv_sems.at[hop],
            device_id={"tile": target},
            device_id_type=MESH,
        )
        copy.start()
        copies.append(copy)
    columns[tile_here] = beam[tile_here]
    write_taps(extent, rate, scale, tap_ref, KMAX // 2 - pulses)
    taps = tap_ref[...]
    response = jnp.dot(spectrum[0], taps, preferred_element_type=jnp.float32) + jnp.dot(
        spectrum[1], taps, preferred_element_type=jnp.float32
    )
    for copy in copies:
        copy.wait()
    signal = jnp.concatenate([unpack(columns[tile]) for tile in range(tiles)], 0)
    image = jnp.dot(forward[0], signal, preferred_element_type=jnp.float32) + jnp.dot(
        forward[1], signal, preferred_element_type=jnp.float32
    )
    real, imag = image[:points], image[points:]
    tap_real, tap_imag = response[:points], response[points:]
    product = jnp.concatenate(
        [real * tap_real - imag * tap_imag, real * tap_imag + imag * tap_real], 0
    )
    high = product.astype(jnp.bfloat16)
    low = (product - high.astype(jnp.float32)).astype(jnp.bfloat16)
    over = (((0,), (0,)), ((), ()))
    result = lax.dot_general(high, inverse[0], over, preferred_element_type=jnp.float32)
    result += lax.dot_general(low, inverse[0], over, preferred_element_type=jnp.float32)
    result += lax.dot_general(high, inverse[1], over, preferred_element_type=jnp.float32)
    out_ref[:, 0, :] = result[:slots, :pulses]
    out_ref[:, 1, :] = result[:slots, pulses:]


def focus_call(raw_echoes, range_taps, beam_weights, order, cells, counts, rates, half_cap):
    local, local_chans, _, cell_count = raw_echoes.shape
    tiles = cells.shape[0]
    pulses = tiles * local
    rows = 2 * local
    out_blocks = cell_count // BLOCK
    tables = [jnp.asarray(table) for table in fourier_tables(pulses)]
    counts, rates = counts[None], rates[None]
    arrays = [raw_echoes, range_taps, beam_weights, counts, rates] + tables
    exchanged = pltpu.VMEM((tiles, 3 * rows // 2, 128), jnp.bfloat16)
    total = pltpu.VMEM((out_blocks, rows, BLOCK), jnp.float32)
    return pl.pallas_call(
        functools.partial(focus_kernel, half_cap),
        out_shape=pltpu.VMEM((half_cap, 2, pulses), jnp.float32),
        in_specs=[pl.BlockSpec(memory_space=pl.ANY)] * (2 + len(arrays)),
        out_specs=pl.BlockSpec(memory_space=pltpu.VMEM),
        scratch_shapes=[pltpu.SMEM(order.shape, order.dtype), pltpu.SMEM(cells.shape, cells.dtype)]
        + [pltpu.VMEM((local_chans, local, 2, cell_count), raw_echoes.dtype)]
        + [pltpu.VMEM(array.shape, array.dtype) for array in arrays[1:]]
        + [
            pltpu.VMEM((out_blocks + 2, rows, BLOCK), jnp.bfloat16),
            pltpu.VMEM((BLOCK, BLOCK), jnp.bfloat16),
            total,
            total,
            pltpu.VMEM((2, tiles, 3 * rows // 2, 128), jnp.bfloat16),
            exchanged,
            exchanged,
            exchanged,
            pltpu.VMEM((4 * pulses, BLOCK), jnp.bfloat16),
            pltpu.SemaphoreType.DMA((len(arrays) + 1,)),
            pltpu.SemaphoreType.DMA((local_chans,)),
            pltpu.SemaphoreType.DMA((2,)),
            pltpu.SemaphoreType.DMA((tiles,)),
            pltpu.SemaphoreType.DMA((tiles,)),
        ],
        compiler_params=pltpu.CompilerParams(
            collective_id=0, has_side_effects=True, vmem_limit_bytes=56 << 20
        ),
    )(order, cells, *arrays)


def on_device(
    raw_echoes, range_taps, beam_weights, channel_order, group_cells, tap_counts, chirp_rates
):
    tiles = group_cells.shape[0]
    local, _, _, cell_count = raw_echoes.shape
    average = cell_count // tiles
    half_cap = (average + average // 2) // lax.axis_size("chan")
    fits = average == BLOCK and lax.axis_size("chan") == 2 and 2 * tiles * local == BLOCK
    if not fits or range_taps.shape[-1] != 2 * BLOCK:
        return generic_device(
            raw_echoes,
            range_taps,
            beam_weights,
            channel_order,
            group_cells,
            tap_counts,
            chirp_rates,
        )
    return focus_call(
        raw_echoes,
        range_taps,
        beam_weights,
        channel_order,
        group_cells,
        tap_counts,
        chirp_rates,
        half_cap,
    )


def solution(mesh):
    return jax.shard_map(
        on_device,
        mesh=mesh,
        in_specs=(P(("scene", "tile"), "chan", None, None), P(), P(), P(), P(), P(), P()),
        out_specs=P(("scene", "tile", "chan"), None, None),
        check_vma=False,
    )
```
